256 devices in a mesh: group: 2 (over x_hi), seq: 8 (over y, core), mp: 16 (over x_lo, z).
Axes of the slice: x: 4 (x_hi: 2, x_lo: 2; x = x_hi * 2 + x_lo), y: 4, z: 8, core: 2. Of those that a mesh axis runs over, the one named last changes fastest.
Arguments:
- image_tokens: bfloat16 [1024, 1280], P(('group', 'seq')), may hold values from -6 to 6
- ln_gain: float32 [1280], replicated, may hold values from 0.25 to 1.75
- ln_bias: float32 [1280], replicated, may hold values from -3 to 3
- mlp_in: bfloat16 [1280, 5120], P(None, 'mp'), may hold values from -0.15625 to 0.15625
- mlp_out: bfloat16 [5120, 1280], P('mp'), may hold values from -0.078125 to 0.078125
- key_proj: bfloat16 [1280, 1024], P(None, 'mp'), may hold values from -0.15625 to 0.15625
- value_proj: bfloat16 [1280, 1024], P(None, 'mp'), may hold values from -0.15625 to 0.15625
- text_tokens: bfloat16 [2048, 4096], P(('group', 'seq')), may hold values from -6 to 6
- text_gain: float32 [4096], replicated, may hold values from 0.25 to 1.75
- query_proj: bfloat16 [4096, 4096], P('seq', 'mp'), may hold values from -0.09375 to 0.09375
- output_proj: bfloat16 [4096, 4096], P('seq', 'mp'), may hold values from -0.09375 to 0.09375
- attn_gate: float32 [1], replicated, may hold values from 0.4 to 1.2
- doc_image: int32 [16], P(('group', 'seq')), may hold values from -1 to 1
- out_cotangent: bfloat16 [2048, 4096], P(('group', 'seq')), may hold values from -6 to 6
Outputs:
- text_out: bfloat16 [2048, 4096], P(('group', 'seq'), 'mp')
- image_grad: float32 [1024, 1280], P(('group', 'seq'))
The draws below stay inside these ranges and needn't reach their ends.
Inputs may be any that keep to these rules, and one draw needn't show every extreme that they name: `doc_image`: entry b names the image that text tokens b * 128 to (b + 1) * 128 - 1 read; -1 means the block reads no image.
All inputs are finite; a program needn't handle non-finite values.
Results may differ from the reference program's by a relative error of at most 0.014.
Values may be sent and summed in bfloat16 or wider, within the bound.
No kernel may reach another device: no remote copies, remote signals or barrier semaphores. Data moves between devices by JAX's collectives and lax.ppermute only.
A program may use at most 64 MiB of HBM per device.

```python
import jax
import jax.numpy as jnp
from jax import lax

DV = 1280
FFV = 5120
DT = 4096
HT = 128
TQH = 32
KVH = 8
BLOCK = 128
IMG_DEV = 64
IMAGE_ROWS = 1024
TEXT = 2048
N_GROUP = 2
N_SEQ = 8


def place_ends(result, stream_key, low, largest):
    longest = result.shape.index(max(result.shape))
    spots = []
    for shift in (0, 1):
        where = [jax.random.randint(jax.random.fold_in(stream_key, axis), (), 0, length) for axis, length in enumerate(result.shape)]
        where[longest] = (where[longest] + shift) % result.shape[longest]
        spots.append(tuple(where))
    return result.at[spots[0]].set(low).at[spots[1]].set(largest)


def block_levels(rng, dims, shards, low, top_value):
    gain, own = 1.0, jax.random.fold_in(rng, 6)
    for dim, parts in shards:
        draws = jnp.exp(jax.random.uniform(jax.random.fold_in(own, dim), (parts,), jnp.float32, low / len(shards), top_value / len(shards)))
        gain = gain * jnp.repeat(draws, dims[dim] // parts).reshape([-1 if axis == dim else 1 for axis in range(len(dims))])
    return gain


def normal_values(rng, shape, deviation, bound, cuts=(), dtype=jnp.bfloat16):
    values = deviation * jax.random.normal(rng, shape, jnp.float32)
    if cuts:
        values = values * block_levels(rng, shape, cuts, -0.22, 0.18)
    return jnp.clip(values, -bound, bound).astype(dtype)


def setup_inputs(seed: int = 0) -> dict:
    arg_keys = jax.random.split(jax.random.key(seed), 15)
    image_tokens = normal_values(arg_keys[0], (IMAGE_ROWS, DV), 1.0, 6.0, ((0, 16),))
    ln_gain = jnp.clip(1.0 + 0.15 * jax.random.normal(arg_keys[1], (DV,), jnp.float32), 0.25, 1.75)
    ln_bias = normal_values(arg_keys[2], (DV,), 0.5, 3.0, (), jnp.float32)
    mlp_in = normal_values(arg_keys[3], (DV, FFV), DV ** -0.5, 0.15625, ((1, 16),))
    mlp_out = normal_values(arg_keys[4], (FFV, DV), FFV ** -0.5, 0.078125, ((0, 16),))
    key_proj = normal_values(arg_keys[5], (DV, KVH * HT), DV ** -0.5, 0.15625, ((1, 16),))
    value_proj = normal_values(arg_keys[6], (DV, KVH * HT), DV ** -0.5, 0.15625, ((1, 16),))
    text_tokens = normal_values(arg_keys[7], (TEXT, DT), 1.0, 6.0, ((0, 16),))
    text_gain = jnp.clip(1.0 + 0.15 * jax.random.normal(arg_keys[8], (DT,), jnp.float32), 0.25, 1.75)
    query_proj = normal_values(arg_keys[9], (DT, TQH * HT), DT ** -0.5, 0.09375, ((0, 8), (1, 16)))
    output_proj = normal_values(arg_keys[10], (DT, TQH * HT), (TQH * HT) ** -0.5, 0.09375, ((0, 8), (1, 16)))
    attn_gate = jnp.clip(jax.random.uniform(arg_keys[11], (1,), jnp.float32, 0.4, 1.2), 0.4, 1.2)
    doc_image = place_ends(jax.random.randint(arg_keys[12], (TEXT // BLOCK,), -1, N_GROUP), jax.random.fold_in(arg_keys[12], 1), -1, N_GROUP - 1).astype(jnp.int32)
    out_cotangent = normal_values(arg_keys[13], (TEXT, DT), 1.0, 6.0, ((0, 16),))
    return {"image_tokens": image_tokens, "ln_gain": ln_gain, "ln_bias": ln_bias, "mlp_in": mlp_in, "mlp_out": mlp_out, "key_proj": key_proj, "value_proj": value_proj, "text_tokens": text_tokens, "text_gain": text_gain, "query_proj": query_proj, "output_proj": output_proj, "attn_gate": attn_gate, "doc_image": doc_image, "out_cotangent": out_cotangent}


EPS_VISION = 1e-06
EPS_TEXT = 1e-05
GELU_COEF = 0.7978845608028654
CUBIC_COEF = 0.044715

def rounded(value):
    return lax.optimization_barrier(value.astype(jnp.bfloat16))

def gelu_parts(pre_act):
    cube_term = pre_act * pre_act * pre_act
    tangent = jnp.tanh(GELU_COEF * (pre_act + CUBIC_COEF * cube_term))
    gelu_value = 0.5 * pre_act * (1.0 + tangent)
    gelu_slope = 0.5 * (1.0 + tangent) + 0.5 * pre_act * (1.0 - tangent * tangent) * GELU_COEF * (1.0 + 3.0 * CUBIC_COEF * pre_act * pre_act)
    return (gelu_value, gelu_slope)

def layer_norm(image_tokens, ln_gain, ln_bias):
    image_float = image_tokens.astype(jnp.float32)
    centred = image_float - lax.optimization_barrier(jnp.mean(image_float, axis=1, keepdims=True))
    inv_scale = lax.rsqrt(lax.optimization_barrier(jnp.mean(centred * centred, axis=1, keepdims=True)) + EPS_VISION)
    normed_hat = centred * inv_scale
    normed = (normed_hat * ln_gain + ln_bias).astype(jnp.bfloat16)
    return (image_float, normed_hat, inv_scale, normed)

def norm_backward(d_normed, normed_hat, inv_scale, ln_gain):
    scaled = d_normed * ln_gain
    first_mean = lax.optimization_barrier(jnp.mean(scaled, axis=1, keepdims=True))
    second_mean = lax.optimization_barrier(jnp.mean(scaled * normed_hat, axis=1, keepdims=True))
    return inv_scale * (scaled - first_mean - normed_hat * second_mean)

def contract_last(left, right):
    return lax.dot_general(left, right, (((1,), (1,)), ((), ())), preferred_element_type=jnp.float32)

def reference(image_tokens, ln_gain, ln_bias, mlp_in, mlp_out, key_proj, value_proj, text_tokens, text_gain, query_proj, output_proj, attn_gate, doc_image, out_cotangent):
    highest = lax.Precision.HIGHEST
    image_float, normed_hat, inv_scale, normed = layer_norm(image_tokens, ln_gain, ln_bias)
    pre_act = jnp.dot(normed, mlp_in, preferred_element_type=jnp.float32)
    gelu_value, gelu_slope = gelu_parts(pre_act)
    hidden_act = gelu_value.astype(jnp.bfloat16)
    image_state = (image_float + jnp.dot(hidden_act, mlp_out, preferred_element_type=jnp.float32)).astype(jnp.bfloat16)
    image_keys = rounded(jnp.dot(image_state, key_proj, preferred_element_type=jnp.float32)).astype(jnp.float32).reshape(-1, KVH, HT)
    image_values = rounded(jnp.dot(image_state, value_proj, preferred_element_type=jnp.float32)).astype(jnp.float32).reshape(-1, KVH, HT)
    text_float = text_tokens.astype(jnp.float32)
    text_scale = lax.rsqrt(lax.optimization_barrier(jnp.mean(text_float * text_float, axis=1, keepdims=True)) + EPS_TEXT)
    text_normed = (text_float * text_scale * text_gain).astype(jnp.bfloat16)
    queries = rounded(jnp.dot(text_normed, query_proj, preferred_element_type=jnp.float32)).astype(jnp.float32)
    gate_factor = jnp.tanh(attn_gate[0])
    has_image = (jnp.repeat(doc_image, BLOCK) >= 0).astype(jnp.float32)[:, None]
    d_proj = (gate_factor * has_image * out_cotangent.astype(jnp.float32)).astype(jnp.bfloat16)
    d_attended = rounded(jnp.dot(d_proj, output_proj, preferred_element_type=jnp.float32)).astype(jnp.float32)
    image_len = IMG_DEV * N_SEQ
    block_count = doc_image.shape[0]
    group_size = TQH // KVH
    head_scale = HT ** (-0.5)

    def block_step(carry, inputs):
        key_grads, value_grads = carry
        block_query, block_grad, block_doc = inputs
        chosen = (jnp.maximum(block_doc, 0) * image_len).astype(jnp.int32)
        key_rows = lax.dynamic_slice_in_dim(image_keys, chosen, image_len, 0)
        value_rows = lax.dynamic_slice_in_dim(image_values, chosen, image_len, 0)
        query_heads = block_query.reshape(BLOCK, KVH, group_size, HT)
        grad_heads = block_grad.reshape(BLOCK, KVH, group_size, HT)
        scores = jnp.einsum('tkgd,skd->kgts', query_heads, key_rows, precision=highest) * head_scale
        top_score = lax.optimization_barrier(jnp.max(scores, axis=3, keepdims=True))
        expo_term = jnp.exp(scores - top_score)
        soft_probs = expo_term / lax.optimization_barrier(jnp.sum(expo_term, axis=3, keepdims=True))
        probs_half = rounded(soft_probs).astype(jnp.float32)
        attended = rounded(jnp.einsum('kgts,skd->tkgd', probs_half, value_rows, precision=highest))
        delta_term = lax.optimization_barrier(jnp.sum(grad_heads * attended.astype(jnp.float32), axis=3))
        d_probs = jnp.einsum('tkgd,skd->kgts', grad_heads, value_rows, precision=highest)
        d_scores = rounded(soft_probs * (d_probs - jnp.transpose(delta_term, (1, 2, 0))[..., None])).astype(jnp.float32)
        value_part = jnp.einsum('kgts,tkgd->skd', probs_half, grad_heads, precision=highest)
        key_part = jnp.einsum('kgts,tkgd->skd', d_scores, query_heads, precision=highest) * head_scale
        old_keys = lax.dynamic_slice_in_dim(key_grads, chosen, image_len, 0)
        old_values = lax.dynamic_slice_in_dim(value_grads, chosen, image_len, 0)
        key_grads = lax.dynamic_update_slice_in_dim(key_grads, old_keys + key_part, chosen, 0)
        value_grads = lax.dynamic_update_slice_in_dim(value_grads, old_values + value_part, chosen, 0)
        return ((key_grads, value_grads), attended.reshape(BLOCK, TQH * HT))
    initial = (jnp.zeros((N_GROUP * image_len, KVH, HT), jnp.float32), jnp.zeros((N_GROUP * image_len, KVH, HT), jnp.float32))
    scanned = (queries.reshape(block_count, BLOCK, TQH * HT), d_attended.reshape(block_count, BLOCK, TQH * HT), doc_image)
    (key_grads, value_grads), attended_blocks = lax.scan(block_step, initial, scanned)
    attended_all = attended_blocks.reshape(-1, TQH * HT)
    text_term = contract_last(attended_all, output_proj)
    text_out = (text_float + gate_factor * has_image * text_term).astype(jnp.bfloat16)
    key_flat = key_grads.reshape(-1, KVH * HT)
    value_flat = value_grads.reshape(-1, KVH * HT)
    state_grad = jnp.dot(key_flat, key_proj.astype(jnp.float32).T, precision=highest) + jnp.dot(value_flat, value_proj.astype(jnp.float32).T, precision=highest)
    d_hidden = contract_last(state_grad.astype(jnp.bfloat16), mlp_out)
    d_pre = (d_hidden * gelu_slope).astype(jnp.bfloat16)
    d_normed = contract_last(d_pre, mlp_in)
    image_grad = state_grad + norm_backward(d_normed, normed_hat, inv_scale, ln_gain)
    return (text_out, image_grad)
```

```python
import jax
import jax.numpy as jnp
from jax import lax
from jax.experimental import pallas as pl
from jax.experimental.pallas import tpu as pltpu
from jax.sharding import PartitionSpec as P

HT = 128
BLOCK = 128
EPS_VISION = 1e-06
EPS_TEXT = 1e-05
GELU_COEF = 0.7978845608028654
CUBIC_COEF = 0.044715

NEAR = (1, 8, 9)
FAR = (2, 4, 6)


F32 = jnp.float32
BF16 = jnp.bfloat16


def swapped(x, axis, mask):
    return lax.ppermute(x, axis, [(i, i ^ mask) for i in range(lax.axis_size(axis))])


def gelu_parts(pre_act):
    cube_term = pre_act * pre_act * pre_act
    tangent = jnp.tanh(GELU_COEF * (pre_act + CUBIC_COEF * cube_term))
    gelu_value = 0.5 * pre_act * (1.0 + tangent)
    gelu_slope = 0.5 * (1.0 + tangent) + 0.5 * pre_act * (1.0 - tangent * tangent) * GELU_COEF * (
        1.0 + 3.0 * CUBIC_COEF * pre_act * pre_act
    )
    return (gelu_value, gelu_slope)


def layer_norm(image_tokens, ln_gain, ln_bias):
    image_float = image_tokens.astype(F32)
    centred = image_float - jnp.mean(image_float, axis=1, keepdims=True)
    inv_scale = lax.rsqrt(jnp.mean(centred * centred, axis=1, keepdims=True) + EPS_VISION)
    normed_hat = centred * inv_scale
    normed = (normed_hat * ln_gain + ln_bias).astype(BF16)
    return (image_float, normed_hat, inv_scale, normed)


def norm_backward(d_normed, normed_hat, inv_scale, ln_gain):
    scaled = d_normed * ln_gain
    first_mean = jnp.mean(scaled, axis=1, keepdims=True)
    second_mean = jnp.mean(scaled * normed_hat, axis=1, keepdims=True)
    return inv_scale * (scaled - first_mean - normed_hat * second_mean)


def contract_last(left, right):
    return lax.dot_general(left, right, (((1,), (1,)), ((), ())), preferred_element_type=F32)


def reduced_chunk(term):
    near = [swapped(term[k].astype(BF16), "mp", NEAR[k - 1]).astype(F32) for k in (1, 2, 3)]
    part = ((term[0] + near[0]) + (near[1] + near[2])).astype(BF16)
    far = [swapped(part, "mp", mask).astype(F32) for mask in FAR]
    return (part.astype(F32) + far[0]) + (far[1] + far[2])


def gathered_chunks(chunk):
    return jnp.stack([chunk] + [swapped(chunk, "mp", mask) for mask in NEAR])


def text_kernel(doc, gate, tokens, gain, cot, *refs):
    pieces, (q_out, d_out, normed, d_proj) = refs[:-4], refs[-4:]
    s = lax.axis_index("seq")
    x = tokens[...].astype(F32)
    scale = lax.rsqrt(jnp.mean(x * x, axis=1, keepdims=True) + EPS_TEXT)
    normed[...] = (x * scale * gain[...]).astype(BF16)
    has_image = jnp.where(doc[0] >= 0, 1.0, 0.0)
    d_proj[...] = (jnp.tanh(gate[...]) * has_image * cot[...].astype(F32)).astype(BF16)
    rows, depth = tokens.shape[0], pieces[0].shape[0]
    total_q = jnp.zeros((rows, q_out.shape[1]), F32)
    total_d = jnp.zeros((rows, d_out.shape[1]), F32)
    for j in range(len(pieces) // 2):
        cols = pl.ds(pl.multiple_of((s ^ j) * depth, depth), depth)
        total_q += jnp.dot(normed[:, cols], pieces[2 * j][...], preferred_element_type=F32)
        total_d += jnp.dot(d_proj[:, cols], pieces[2 * j + 1][...], preferred_element_type=F32)
    q_out[...] = total_q.astype(BF16)
    d_out[...] = total_d.astype(BF16)


def attend_kernel(doc, q, d, own, other, att_out, g_own, g_other):
    r = jnp.maximum(doc[0], 0) ^ lax.axis_index("group")
    peers, _, image_rows, _ = own.shape
    blocks = [ref[k, r] for ref in (own, other) for k in range(peers)]
    keys = jnp.concatenate([b[:, :HT] for b in blocks], axis=0)
    values = jnp.concatenate([b[:, HT:] for b in blocks], axis=0)
    head_scale = HT ** (-0.5)
    key_grads = jnp.zeros(keys.shape, F32)
    value_grads = jnp.zeros(keys.shape, F32)
    for h in range(q.shape[1] // HT):
        cols = slice(h * HT, (h + 1) * HT)
        qh, dh = q[:, cols], d[:, cols]
        scores = contract_last(keys, qh) * head_scale
        expo = jnp.exp(scores - jnp.max(scores, axis=0, keepdims=True))
        soft = expo / jnp.sum(expo, axis=0, keepdims=True)
        half = soft.astype(BF16)
        att = lax.dot_general(half, values, (((0,), (0,)), ((), ())), preferred_element_type=F32)
        att_out[:, cols] = att.astype(BF16)
        d_probs = contract_last(values, dh)
        delta = jnp.sum(half.astype(F32) * d_probs, axis=0, keepdims=True)
        d_scores = (soft * (d_probs - delta)).astype(BF16)
        value_grads += jnp.dot(half, dh, preferred_element_type=F32)
        key_grads += jnp.dot(d_scores, qh, preferred_element_type=F32)
    grads = jnp.concatenate([key_grads * head_scale, value_grads], axis=1).astype(BF16)
    nothing = jnp.zeros((image_rows, 2 * HT), BF16)
    for i, ref in enumerate((g_own, g_other)):
        for k in range(peers):
            at = (i * peers + k) * image_rows
            ref[k, r] = grads[at : at + image_rows]
            ref[k, 1 - r] = nothing


def term_kernel(att, *refs):
    pieces, out = refs[:-1], refs[-1]
    s, m = lax.axis_index("seq"), lax.axis_index("mp")
    width = out.shape[2]
    for j, piece in enumerate(pieces):
        term = contract_last(att[...], piece[...]).astype(BF16)
        for half in range(piece.shape[0] // width):
            mask = ((s ^ j) * (piece.shape[0] // width) + half) ^ m
            near = (mask & 1) | ((mask >> 3) << 1)
            far = (mask >> 1) & 3
            out[near * 4 + far] = term[:, half * width : (half + 1) * width]


VMEM = pl.BlockSpec(memory_space=pltpu.VMEM)
SMEM = pl.BlockSpec(memory_space=pltpu.SMEM)


def shards(
    image_tokens,
    ln_gain,
    ln_bias,
    mlp_in,
    mlp_out,
    key_proj,
    value_proj,
    text_tokens,
    text_gain,
    query_proj,
    output_proj,
    attn_gate,
    doc_image,
    out_cotangent,
):
    m = lax.axis_index("mp")
    image_rows, vision_width = image_tokens.shape
    text_rows, text_width = text_tokens.shape
    out_width = text_width // lax.axis_size("mp")
    near_index = (m & 1) | ((m >> 3) << 1)
    chunk_rows = image_rows // 4

    w = jnp.concatenate([query_proj, output_proj], axis=0)
    depth = query_proj.shape[0]
    w1, w3 = swapped(w, "seq", 2), swapped(w, "seq", 6)
    w2q, w2o = swapped(w1[:depth], "seq", 6), swapped(w3[depth:], "seq", 2)
    by_y = [(query_proj, output_proj), (w1[:depth], w1[depth:]), (w2q, w2o), (w3[:depth], w3[depth:])]
    v0, v1, v3 = [swapped(x, "seq", 1) for x in (w, w1, w3)]
    v2q, v2o = swapped(w2q, "seq", 1), swapped(w2o, "seq", 1)
    by_y_other = [(v0[:depth], v0[depth:]), (v1[:depth], v1[depth:]), (v2q, v2o), (v3[:depth], v3[depth:])]
    pairs = [pair for k in range(4) for pair in (by_y[k], by_y_other[k])]

    lines = image_tokens.reshape(4, chunk_rows, vision_width)
    ordered = jnp.concatenate(
        [lax.dynamic_slice_in_dim(lines, near_index ^ k, 1, 0) for k in range(4)], axis=0
    ).reshape(image_rows, vision_width)
    image_float, normed_hat, inv_scale, normed = layer_norm(ordered, ln_gain, ln_bias)
    pre_act = jnp.dot(normed, mlp_in, preferred_element_type=F32)
    gelu_value, gelu_slope = gelu_parts(pre_act)
    mlp_term = jnp.dot(gelu_value.astype(BF16), mlp_out, preferred_element_type=F32)
    mlp_chunk = reduced_chunk(mlp_term.reshape(4, chunk_rows, vision_width))
    state_chunk = (image_float[:chunk_rows] + mlp_chunk).astype(BF16)
    image_state = gathered_chunks(state_chunk).reshape(image_rows, vision_width)

    own_kv = jnp.stack([key_proj, value_proj])
    partner_kv = swapped(own_kv, "mp", 1)
    is_odd = m % 2 == 1
    first, second = jnp.where(is_odd, partner_kv, own_kv), jnp.where(is_odd, own_kv, partner_kv)
    kv_cols = jnp.concatenate([first[0], second[0], first[1], second[1]], axis=1)
    local_kv = jnp.dot(image_state, kv_cols, preferred_element_type=F32).astype(BF16)
    both = jnp.stack([local_kv, swapped(local_kv, "group", 1)])
    own_core = jnp.stack([both] + [swapped(both, "seq", 2 * k) for k in (1, 2, 3)])
    other_core = swapped(own_core, "seq", 1)

    head_cols = query_proj.shape[1]
    small = jax.ShapeDtypeStruct((text_rows, head_cols), BF16)
    queries, d_attended = pl.pallas_call(
        text_kernel,
        out_shape=(small, small),
        in_specs=[SMEM] + [VMEM] * (4 + 2 * len(pairs)),
        out_specs=(VMEM, VMEM),
        scratch_shapes=[pltpu.VMEM((text_rows, text_width), BF16)] * 2,
        name="text_projections",
    )(
        doc_image,
        attn_gate.reshape(1, 1),
        text_tokens,
        text_gain.reshape(1, text_width),
        out_cotangent,
        *[x for pair in pairs for x in pair],
    )

    grid = jax.ShapeDtypeStruct(own_core.shape, BF16)
    attended, grads_own, grads_other = pl.pallas_call(
        attend_kernel,
        out_shape=(small, grid, grid),
        in_specs=[SMEM] + [VMEM] * 4,
        out_specs=(VMEM, VMEM, VMEM),
        name="attention",
    )(doc_image, queries, d_attended, own_core, other_core)

    summed = (grads_own.astype(F32) + swapped(grads_other, "seq", 1).astype(F32)).astype(BF16)
    along_y = [swapped(summed[k], "seq", 2 * k).astype(F32) for k in (1, 2, 3)]
    summed = (summed[0].astype(F32) + along_y[0]) + (along_y[1] + along_y[2])
    kv_grads = summed[0] + swapped(summed[1].astype(BF16), "group", 1).astype(F32)
    state_term = contract_last(kv_grads.astype(BF16), kv_cols)
    state_chunk_grad = reduced_chunk(state_term.reshape(4, chunk_rows, vision_width))
    state_half = gathered_chunks(state_chunk_grad.astype(BF16)).reshape(image_rows, vision_width)
    d_hidden = contract_last(state_half, mlp_out)
    d_pre = (d_hidden * gelu_slope).astype(BF16)
    normed_term = contract_last(d_pre, mlp_in)
    d_normed = reduced_chunk(normed_term.reshape(4, chunk_rows, vision_width))
    grad_chunk = state_chunk_grad + norm_backward(
        d_normed, normed_hat[:chunk_rows], inv_scale[:chunk_rows], ln_gain
    )
    grads = gathered_chunks(grad_chunk.astype(BF16))
    image_grad = jnp.concatenate(
        [lax.dynamic_slice_in_dim(grads, near_index ^ k, 1, 0) for k in range(4)], axis=0
    ).reshape(image_rows, vision_width).astype(F32)

    terms = pl.pallas_call(
        term_kernel,
        out_shape=jax.ShapeDtypeStruct((16, text_rows, out_width), BF16),
        in_specs=[VMEM] * (1 + len(pairs)),
        out_specs=VMEM,
        name="text_terms",
    )(attended, *[pair[1] for pair in pairs])
    terms = terms.reshape(4, 4, text_rows, out_width)
    near = [swapped(terms[k], "mp", NEAR[k - 1]).astype(F32) for k in (1, 2, 3)]
    part = (terms[0].astype(F32) + near[0]) + (near[1] + near[2])
    far = [swapped(part[k].astype(BF16), "mp", FAR[k - 1]).astype(F32) for k in (1, 2, 3)]
    text_share = (part[0] + far[0]) + (far[1] + far[2])
    text_slice = lax.dynamic_slice_in_dim(text_tokens, m * out_width, out_width, 1).astype(F32)
    has_image = jnp.where(doc_image[0] >= 0, 1.0, 0.0)
    text_out = (text_slice + jnp.tanh(attn_gate[0]) * has_image * text_share).astype(BF16)
    return (text_out, image_grad)


def solution(mesh):
    return jax.shard_map(
        shards,
        mesh=mesh,
        in_specs=(
            P(("group", "seq"), None),
            P(),
            P(),
            P(None, "mp"),
            P("mp", None),
            P(None, "mp"),
            P(None, "mp"),
            P(("group", "seq"), None),
            P(),
            P("seq", "mp"),
            P("seq", "mp"),
            P(),
            P(("group", "seq")),
            P(("group", "seq"), None),
        ),
        out_specs=(P(("group", "seq"), "mp"), P(("group", "seq"), None)),
        check_vma=False,
    )
```

```python
import jax
import jax.numpy as jnp
from jax import lax
from jax.experimental import pallas as pl
from jax.experimental.pallas import tpu as pltpu
from jax.sharding import PartitionSpec as P


HT = 128
EPS_VISION = 1e-06
EPS_TEXT = 1e-05
GELU_COEF = 0.7978845608028654
CUBIC_COEF = 0.044715

NEAR = (1, 8, 9)
FAR = (4, 2, 6)
NEAR_SETS = [[b, b + 1, b + 8, b + 9] for b in (0, 2, 4, 6)]
ALONG_Y = [[0, 2, 4, 6], [1, 3, 5, 7]]


F32 = jnp.float32
BF16 = jnp.bfloat16


def exchanged(x, axis, groups):
    return lax.all_to_all(x, axis, 0, 0, tiled=True, axis_index_groups=groups)


def swapped(x, axis, mask):
    return lax.ppermute(x, axis, [(i, i ^ mask) for i in range(lax.axis_size(axis))])


def gelu_parts(pre_act):
    cube_term = pre_act * pre_act * pre_act
    tangent = jnp.tanh(GELU_COEF * (pre_act + CUBIC_COEF * cube_term))
    gelu_value = 0.5 * pre_act * (1.0 + tangent)
    gelu_slope = 0.5 * (1.0 + tangent) + 0.5 * pre_act * (1.0 - tangent * tangent) * GELU_COEF * (
        1.0 + 3.0 * CUBIC_COEF * pre_act * pre_act
    )
    return (gelu_value, gelu_slope)


def layer_norm(image_tokens, ln_gain, ln_bias):
    image_float = image_tokens.astype(F32)
    centred = image_float - jnp.mean(image_float, axis=1, keepdims=True)
    inv_scale = lax.rsqrt(jnp.mean(centred * centred, axis=1, keepdims=True) + EPS_VISION)
    normed_hat = centred * inv_scale
    normed = (normed_hat * ln_gain + ln_bias).astype(BF16)
    return (image_float, normed_hat, inv_scale, normed)


def norm_backward(d_normed, normed_hat, inv_scale, ln_gain):
    scaled = d_normed * ln_gain
    first_mean = jnp.mean(scaled, axis=1, keepdims=True)
    second_mean = jnp.mean(scaled * normed_hat, axis=1, keepdims=True)
    return inv_scale * (scaled - first_mean - normed_hat * second_mean)


def contract_last(left, right):
    return lax.dot_general(left, right, (((1,), (1,)), ((), ())), preferred_element_type=F32)


def reduced_chunk(term):
    near = [swapped(term[k].astype(BF16), "mp", NEAR[k - 1]).astype(F32) for k in (1, 2, 3)]
    part = ((term[0] + near[0]) + (near[1] + near[2])).astype(BF16)
    far = [swapped(part, "mp", mask).astype(F32) for mask in FAR]
    return (part.astype(F32) + far[1]) + (far[0] + far[2])


def gathered_chunks(chunk):
    return jnp.stack([chunk] + [swapped(chunk, "mp", mask) for mask in NEAR])


def spread_kernel(first, second, out, held, sems):
    rows = first.shape[0]
    copies = [
        pltpu.make_async_copy(ref, held.at[pl.ds(i * rows, rows)], sems.at[i])
        for i, ref in enumerate((first, second))
    ]
    for copy in copies:
        copy.start()
    for copy in copies:
        copy.wait()
    copies = [pltpu.make_async_copy(held, out.at[i], sems.at[2 + i]) for i in range(out.shape[0])]
    for copy in copies:
        copy.start()
    for copy in copies:
        copy.wait()


def text_kernel(doc, gate, gain, own, other, tokens_in, cot_in, q_out, d_out, tokens, cot, normed, d_proj, sems):
    copies = [
        pltpu.make_async_copy(tokens_in, tokens, sems.at[0]),
        pltpu.make_async_copy(cot_in, cot, sems.at[1]),
    ]
    for copy in copies:
        copy.start()
    core = lax.axis_index("seq") & 1
    copies[0].wait()
    x = tokens[...].astype(F32)
    scale = lax.rsqrt(jnp.mean(x * x, axis=1, keepdims=True) + EPS_TEXT)
    normed[...] = (x * scale * gain[...]).astype(BF16)
    copies[1].wait()
    has_image = jnp.where(doc[0] >= 0, 1.0, 0.0)
    d_proj[...] = (jnp.tanh(gate[...]) * has_image * cot[...].astype(F32)).astype(BF16)
    rows, depth = tokens.shape[0], own.shape[1] // 2
    total_q = jnp.zeros((rows, q_out.shape[1]), F32)
    total_d = jnp.zeros((rows, d_out.shape[1]), F32)
    for y in range(own.shape[0]):
        for ref, side in ((own, core), (other, 1 - core)):
            cols = pl.ds(pl.multiple_of((2 * y + side) * depth, depth), depth)
            total_q += jnp.dot(normed[:, cols], ref[y, :depth], preferred_element_type=F32)
            total_d += jnp.dot(d_proj[:, cols], ref[y, depth:], preferred_element_type=F32)
    q_out[...] = total_q.astype(BF16)
    d_out[...] = total_d.astype(BF16)


def attend_kernel(doc, q, d, own, other, att_out, g_own, g_other):
    r = jnp.maximum(doc[0], 0) ^ lax.axis_index("group")
    peers, _, image_rows, _ = own.shape
    blocks = [ref[k, r] for ref in (own, other) for k in range(peers)]
    keys = jnp.concatenate([b[:, :HT] for b in blocks], axis=0)
    values = jnp.concatenate([b[:, HT:] for b in blocks], axis=0)
    head_scale = HT ** (-0.5)
    key_grads = jnp.zeros(keys.shape, F32)
    value_grads = jnp.zeros(keys.shape, F32)
    odd = (lax.axis_index("mp") & 1) == 1

    def turned(x):
        return jnp.where(odd, jnp.concatenate([x[:, HT // 2 :], x[:, : HT // 2]], axis=1), x)

    for h in range(q.shape[1] // HT):
        cols = slice(h * HT, (h + 1) * HT)
        qh, dh = turned(q[:, cols]), turned(d[:, cols])
        scores = contract_last(keys, qh) * head_scale
        expo = jnp.exp(scores - jnp.max(scores, axis=0, keepdims=True))
        soft = expo / jnp.sum(expo, axis=0, keepdims=True)
        half = soft.astype(BF16)
        att = lax.dot_general(half, values, (((0,), (0,)), ((), ())), preferred_element_type=F32)
        att_out[:, cols] = turned(att).astype(BF16)
        d_probs = contract_last(values, dh)
        delta = jnp.sum(half.astype(F32) * d_probs, axis=0, keepdims=True)
        d_scores = (soft * (d_probs - delta)).astype(BF16)
        value_grads += jnp.dot(half, dh, preferred_element_type=F32)
        key_grads += jnp.dot(d_scores, qh, preferred_element_type=F32)
    grads = jnp.concatenate([key_grads * head_scale, value_grads], axis=1).astype(BF16)
    nothing = jnp.zeros((image_rows, 2 * HT), BF16)
    for i, ref in enumerate((g_own, g_other)):
        for k in range(peers):
            at = (i * peers + k) * image_rows
            ref[r, k] = grads[at : at + image_rows]
            ref[1 - r, k] = nothing


def term_kernel(att, own, other, out):
    core, m = lax.axis_index("seq") & 1, lax.axis_index("mp")
    depth, width = own.shape[1] // 2, out.shape[2]
    for y in range(own.shape[0]):
        for ref, side in ((own, core), (other, 1 - core)):
            term = contract_last(att[...], ref[y, depth:]).astype(BF16)
            for half in range(depth // width):
                to = (2 * y + side) * (depth // width) + half
                near = (to & 1) | ((to >> 3) << 1)
                out[near * 4 + (((to ^ m) >> 1) & 3)] = term[:, half * width : (half + 1) * width]


def sum_kernel(arrived, kept, sent):
    for k in range(arrived.shape[1]):
        parts = [arrived[i, k].astype(F32) for i in range(arrived.shape[0])]
        total = (parts[0] + parts[1]) + (parts[2] + parts[3])
        if k in (1, 2):
            sent[k - 1] = total.astype(BF16)
        else:
            kept[k // 2] = total


VMEM = pl.BlockSpec(memory_space=pltpu.VMEM)
SMEM = pl.BlockSpec(memory_space=pltpu.SMEM)
HBM = pl.BlockSpec(memory_space=pltpu.HBM)
SMALL_VMEM = pltpu.CompilerParams(vmem_limit_bytes=16 * 1024 * 1024)


def shards(
    image_tokens,
    ln_gain,
    ln_bias,
    mlp_in,
    mlp_out,
    key_proj,
    value_proj,
    text_tokens,
    text_gain,
    query_proj,
    output_proj,
    attn_gate,
    doc_image,
    out_cotangent,
):
    m = lax.axis_index("mp")
    image_rows, vision_width = image_tokens.shape
    text_rows, text_width = text_tokens.shape
    out_width = text_width // lax.axis_size("mp")
    near_index = (m & 1) | ((m >> 3) << 1)
    chunk_rows = image_rows // 4

    depth, head_cols = query_proj.shape
    spread = pl.pallas_call(
        spread_kernel,
        out_shape=jax.ShapeDtypeStruct((4, 2 * depth, head_cols), BF16),
        in_specs=[HBM] * 2,
        out_specs=HBM,
        scratch_shapes=[pltpu.VMEM((2 * depth, head_cols), BF16), pltpu.SemaphoreType.DMA((6,))],
        compiler_params=SMALL_VMEM,
        name="spread",
    )(query_proj, output_proj)
    along = exchanged(spread, "seq", ALONG_Y)
    weights = [along, swapped(along, "seq", 1)]

    lines = image_tokens.reshape(4, chunk_rows, vision_width)
    ordered = jnp.concatenate(
        [lax.dynamic_slice_in_dim(lines, near_index ^ k, 1, 0) for k in range(4)], axis=0
    ).reshape(image_rows, vision_width)
    image_float, normed_hat, inv_scale, normed = layer_norm(ordered, ln_gain, ln_bias)
    pre_act = jnp.dot(normed, mlp_in, preferred_element_type=F32)
    gelu_value, gelu_slope = gelu_parts(pre_act)
    mlp_term = jnp.dot(gelu_value.astype(BF16), mlp_out, preferred_element_type=F32)
    mlp_chunk = reduced_chunk(mlp_term.reshape(4, chunk_rows, vision_width))
    state_chunk = (image_float[:chunk_rows] + mlp_chunk).astype(BF16)
    image_state = gathered_chunks(state_chunk).reshape(image_rows, vision_width)

    partner_kv = swapped(jnp.stack([key_proj, value_proj]), "mp", 1)
    kv_cols = jnp.concatenate([key_proj, partner_kv[0], value_proj, partner_kv[1]], axis=1)
    local_kv = jnp.dot(image_state, kv_cols, preferred_element_type=F32).astype(BF16)
    both = jnp.stack([local_kv, swapped(local_kv, "group", 1)])
    own_core = jnp.stack([both] + [swapped(both, "seq", 2 * k) for k in (1, 2, 3)])
    other_core = swapped(own_core, "seq", 1)

    small = jax.ShapeDtypeStruct((text_rows, head_cols), BF16)
    wide = pltpu.VMEM((text_rows, text_width), BF16)
    queries, d_attended = pl.pallas_call(
        text_kernel,
        out_shape=(small, small),
        in_specs=[SMEM] + [VMEM] * 4 + [HBM] * 2,
        out_specs=(VMEM, VMEM),
        scratch_shapes=[wide] * 4 + [pltpu.SemaphoreType.DMA((2,))],
        compiler_params=SMALL_VMEM,
        name="text_projections",
    )(
        doc_image,
        attn_gate.reshape(1, 1),
        text_gain.reshape(1, text_width),
        *weights,
        *[pltpu.with_memory_space_constraint(x, pltpu.HBM) for x in (text_tokens, out_cotangent)],
    )

    grid = jax.ShapeDtypeStruct((2, 4, image_rows, 2 * HT), BF16)
    attended, grads_own, grads_other = pl.pallas_call(
        attend_kernel,
        out_shape=(small, grid, grid),
        in_specs=[SMEM] + [VMEM] * 4,
        out_specs=(VMEM, VMEM, VMEM),
        compiler_params=SMALL_VMEM,
        name="attention",
    )(doc_image, queries, d_attended, own_core, other_core)

    summed = grads_own.astype(F32) + swapped(grads_other, "seq", 1).astype(F32)
    summed = summed[0] + swapped(summed[1].astype(BF16), "group", 1).astype(F32)
    along_y = [swapped(summed[k].astype(BF16), "seq", 2 * k).astype(F32) for k in (1, 2, 3)]
    kv_grads = (summed[0] + along_y[0]) + (along_y[1] + along_y[2])
    state_term = contract_last(kv_grads.astype(BF16), kv_cols)
    state_chunk_grad = reduced_chunk(state_term.reshape(4, chunk_rows, vision_width))
    state_half = gathered_chunks(state_chunk_grad.astype(BF16)).reshape(image_rows, vision_width)
    d_hidden = contract_last(state_half, mlp_out)
    d_pre = (d_hidden * gelu_slope).astype(BF16)
    normed_term = contract_last(d_pre, mlp_in)
    d_normed = reduced_chunk(normed_term.reshape(4, chunk_rows, vision_width))
    grad_chunk = state_chunk_grad + norm_backward(
        d_normed, normed_hat[:chunk_rows], inv_scale[:chunk_rows], ln_gain
    )
    grads = gathered_chunks(grad_chunk.astype(BF16))
    image_grad = jnp.concatenate(
        [lax.dynamic_slice_in_dim(grads, near_index ^ k, 1, 0) for k in range(4)], axis=0
    ).reshape(image_rows, vision_width).astype(F32)

    terms = pl.pallas_call(
        term_kernel,
        out_shape=jax.ShapeDtypeStruct((16, text_rows, out_width), BF16),
        in_specs=[VMEM] * 3,
        out_specs=VMEM,
        compiler_params=SMALL_VMEM,
        name="text_terms",
    )(attended, *weights)
    terms = terms.reshape(4, 4, text_rows, out_width)
    kept, sent = pl.pallas_call(
        sum_kernel,
        out_shape=(
            jax.ShapeDtypeStruct((2, text_rows, out_width), F32),
            jax.ShapeDtypeStruct((2, text_rows, out_width), BF16),
        ),
        in_specs=[VMEM],
        out_specs=(VMEM, VMEM),
        compiler_params=SMALL_VMEM,
        name="near_sum",
    )(exchanged(terms, "mp", NEAR_SETS))
    passed = swapped(sent, "mp", 2).astype(F32)
    last = swapped((kept[1] + passed[1]).astype(BF16), "mp", 6).astype(F32)
    text_share = kept[0] + passed[0] + last
    text_slice = lax.dynamic_slice_in_dim(text_tokens, m * out_width, out_width, 1).astype(F32)
    has_image = jnp.where(doc_image[0] >= 0, 1.0, 0.0)
    text_out = (text_slice + jnp.tanh(attn_gate[0]) * has_image * text_share).astype(BF16)
    return (text_out, image_grad)


def solution(mesh):
    return jax.shard_map(
        shards,
        mesh=mesh,
        in_specs=(
            P(("group", "seq"), None),
            P(),
            P(),
            P(None, "mp"),
            P("mp", None),
            P(None, "mp"),
            P(None, "mp"),
            P(("group", "seq"), None),
            P(),
            P("seq", "mp"),
            P("seq", "mp"),
            P(),
            P(("group", "seq")),
            P(("group", "seq"), None),
        ),
        out_specs=(P(("group", "seq"), "mp"), P(("group", "seq"), None)),
        check_vma=False,
    )
```

```python
import jax
import jax.numpy as jnp
from jax import lax
from jax.experimental import pallas as pl
from jax.experimental.pallas import tpu as pltpu
from jax.sharding import PartitionSpec as P


HT = 128
EPS_VISION = 1e-06
EPS_TEXT = 1e-05
GELU_COEF = 0.7978845608028654
CUBIC_COEF = 0.044715

NEAR = (1, 8, 9)
FAR = (4, 2, 6)
FARTHEST_NEAR = (3, 1, 2)
FARTHEST_Y = (2, 1, 3)
NEAR_SETS = [[b, b + 1, b + 8, b + 9] for b in (0, 2, 4, 6)]
ALONG_Y = [[0, 2, 4, 6], [1, 3, 5, 7]]


F32 = jnp.float32
BF16 = jnp.bfloat16


def exchanged(x, axis, groups):
    return lax.all_to_all(x, axis, 0, 0, tiled=True, axis_index_groups=groups)


def swapped(x, axis, mask):
    return lax.ppermute(x, axis, [(i, i ^ mask) for i in range(lax.axis_size(axis))])


def gelu_parts(pre_act):
    cube_term = pre_act * pre_act * pre_act
    tangent = jnp.tanh(GELU_COEF * (pre_act + CUBIC_COEF * cube_term))
    gelu_value = 0.5 * pre_act * (1.0 + tangent)
    gelu_slope = 0.5 * (1.0 + tangent) + 0.5 * pre_act * (1.0 - tangent * tangent) * GELU_COEF * (
        1.0 + 3.0 * CUBIC_COEF * pre_act * pre_act
    )
    return (gelu_value, gelu_slope)


def layer_norm(image_tokens, ln_gain, ln_bias):
    image_float = image_tokens.astype(F32)
    centred = image_float - jnp.mean(image_float, axis=1, keepdims=True)
    inv_scale = lax.rsqrt(jnp.mean(centred * centred, axis=1, keepdims=True) + EPS_VISION)
    normed_hat = centred * inv_scale
    normed = (normed_hat * ln_gain + ln_bias).astype(BF16)
    return (image_float, normed_hat, inv_scale, normed)


def norm_backward(d_normed, normed_hat, inv_scale, ln_gain):
    scaled = d_normed * ln_gain
    first_mean = jnp.mean(scaled, axis=1, keepdims=True)
    second_mean = jnp.mean(scaled * normed_hat, axis=1, keepdims=True)
    return inv_scale * (scaled - first_mean - normed_hat * second_mean)


def contract_last(left, right):
    return lax.dot_general(left, right, (((1,), (1,)), ((), ())), preferred_element_type=F32)


def reduced_chunk(term):
    near = {k: swapped(term[k].astype(BF16), "mp", NEAR[k - 1]).astype(F32) for k in FARTHEST_NEAR}
    part = ((term[0] + near[1]) + (near[2] + near[3])).astype(BF16)
    far = [swapped(part, "mp", mask).astype(F32) for mask in FAR]
    return (part.astype(F32) + far[1]) + (far[0] + far[2])


def gathered_chunks(chunk):
    near = {k: swapped(chunk, "mp", NEAR[k - 1]) for k in FARTHEST_NEAR}
    return jnp.stack([chunk, near[1], near[2], near[3]])


def spread_kernel(first, second, out, held, sems):
    rows = first.shape[0]
    copies = [
        pltpu.make_async_copy(ref, held.at[pl.ds(i * rows, rows)], sems.at[i])
        for i, ref in enumerate((first, second))
    ]
    for copy in copies:
        copy.start()
    for copy in copies:
        copy.wait()
    copies = [pltpu.make_async_copy(held, out.at[i], sems.at[2 + i]) for i in range(out.shape[0])]
    for copy in copies:
        copy.start()
    for copy in copies:
        copy.wait()


def text_kernel(doc, gate, gain, own, other, tokens_in, cot_in, q_out, d_out, tokens, cot, normed, d_proj, sems):
    copies = [
        pltpu.make_async_copy(tokens_in, tokens, sems.at[0]),
        pltpu.make_async_copy(cot_in, cot, sems.at[1]),
    ]
    for copy in copies:
        copy.start()
    core = lax.axis_index("seq") & 1
    copies[0].wait()
    x = tokens[...].astype(F32)
    scale = lax.rsqrt(jnp.mean(x * x, axis=1, keepdims=True) + EPS_TEXT)
    normed[...] = (x * scale * gain[...]).astype(BF16)
    copies[1].wait()
    has_image = jnp.where(doc[0] >= 0, 1.0, 0.0)
    d_proj[...] = (jnp.tanh(gate[...]) * has_image * cot[...].astype(F32)).astype(BF16)
    rows, depth = tokens.shape[0], own.shape[1] // 2
    total_q = jnp.zeros((rows, q_out.shape[1]), F32)
    total_d = jnp.zeros((rows, d_out.shape[1]), F32)
    for y in range(own.shape[0]):
        for ref, side in ((own, core), (other, 1 - core)):
            cols = pl.ds(pl.multiple_of((2 * y + side) * depth, depth), depth)
            total_q += jnp.dot(normed[:, cols], ref[y, :depth], preferred_element_type=F32)
            total_d += jnp.dot(d_proj[:, cols], ref[y, depth:], preferred_element_type=F32)
    q_out[...] = total_q.astype(BF16)
    d_out[...] = total_d.astype(BF16)


def attend_kernel(doc, q, d, own, other, att_out, g_own, g_other):
    r = jnp.maximum(doc[0], 0) ^ lax.axis_index("group")
    peers, _, image_rows, _ = own.shape
    blocks = [ref[k, r] for ref in (own, other) for k in range(peers)]
    keys = jnp.concatenate([b[:, :HT] for b in blocks], axis=0)
    values = jnp.concatenate([b[:, HT:] for b in blocks], axis=0)
    head_scale = HT ** (-0.5)
    key_grads = jnp.zeros(keys.shape, F32)
    value_grads = jnp.zeros(keys.shape, F32)
    odd = (lax.axis_index("mp") & 1) == 1

    def turned(x):
        return jnp.where(odd, jnp.concatenate([x[:, HT // 2 :], x[:, : HT // 2]], axis=1), x)

    for h in range(q.shape[1] // HT):
        cols = slice(h * HT, (h + 1) * HT)
        qh, dh = turned(q[:, cols]), turned(d[:, cols])
        scores = contract_last(keys, qh) * head_scale
        expo = jnp.exp(scores - jnp.max(scores, axis=0, keepdims=True))
        soft = expo / jnp.sum(expo, axis=0, keepdims=True)
        half = soft.astype(BF16)
        att = lax.dot_general(half, values, (((0,), (0,)), ((), ())), preferred_element_type=F32)
        att_out[:, cols] = turned(att).astype(BF16)
        d_probs = contract_last(values, dh)
        delta = jnp.sum(half.astype(F32) * d_probs, axis=0, keepdims=True)
        d_scores = (soft * (d_probs - delta)).astype(BF16)
        value_grads += jnp.dot(half, dh, preferred_element_type=F32)
        key_grads += jnp.dot(d_scores, qh, preferred_element_type=F32)
    grads = jnp.concatenate([key_grads * head_scale, value_grads], axis=1).astype(BF16)
    nothing = jnp.zeros((image_rows, 2 * HT), BF16)
    for i, ref in enumerate((g_own, g_other)):
        for k in range(peers):
            at = (i * peers + k) * image_rows
            ref[r, k] = grads[at : at + image_rows]
            ref[1 - r, k] = nothing


def term_kernel(att, own, other, out):
    core, m = lax.axis_index("seq") & 1, lax.axis_index("mp")
    depth, width = own.shape[1] // 2, out.shape[2]
    for y in range(own.shape[0]):
        for ref, side in ((own, core), (other, 1 - core)):
            term = contract_last(att[...], ref[y, depth:]).astype(BF16)
            for half in range(depth // width):
                to = (2 * y + side) * (depth // width) + half
                near = (to & 1) | ((to >> 3) << 1)
                out[near * 4 + (((to ^ m) >> 1) & 3)] = term[:, half * width : (half + 1) * width]


def sum_kernel(arrived, kept, sent):
    for k in range(arrived.shape[1]):
        parts = [arrived[i, k].astype(F32) for i in range(arrived.shape[0])]
        total = (parts[0] + parts[1]) + (parts[2] + parts[3])
        if k in (1, 2):
            sent[k - 1] = total.astype(BF16)
        else:
            kept[k // 2] = total


VMEM = pl.BlockSpec(memory_space=pltpu.VMEM)
SMEM = pl.BlockSpec(memory_space=pltpu.SMEM)
HBM = pl.BlockSpec(memory_space=pltpu.HBM)
SMALL_VMEM = pltpu.CompilerParams(vmem_limit_bytes=16 * 1024 * 1024)


def shards(
    image_tokens,
    ln_gain,
    ln_bias,
    mlp_in,
    mlp_out,
    key_proj,
    value_proj,
    text_tokens,
    text_gain,
    query_proj,
    output_proj,
    attn_gate,
    doc_image,
    out_cotangent,
):
    m = lax.axis_index("mp")
    image_rows, vision_width = image_tokens.shape
    text_rows, text_width = text_tokens.shape
    out_width = text_width // lax.axis_size("mp")
    near_index = (m & 1) | ((m >> 3) << 1)
    chunk_rows = image_rows // 4

    depth, head_cols = query_proj.shape
    spread = pl.pallas_call(
        spread_kernel,
        out_shape=jax.ShapeDtypeStruct((4, 2 * depth, head_cols), BF16),
        in_specs=[HBM] * 2,
        out_specs=HBM,
        scratch_shapes=[pltpu.VMEM((2 * depth, head_cols), BF16), pltpu.SemaphoreType.DMA((6,))],
        compiler_params=SMALL_VMEM,
        name="spread",
    )(query_proj, output_proj)
    along = exchanged(spread, "seq", ALONG_Y)
    weights = [along, swapped(along, "seq", 1)]

    lines = image_tokens.reshape(4, chunk_rows, vision_width)
    ordered = jnp.concatenate(
        [lax.dynamic_slice_in_dim(lines, near_index ^ k, 1, 0) for k in range(4)], axis=0
    ).reshape(image_rows, vision_width)
    image_float, normed_hat, inv_scale, normed = layer_norm(ordered, ln_gain, ln_bias)
    pre_act = jnp.dot(normed, mlp_in, preferred_element_type=F32)
    gelu_value, gelu_slope = gelu_parts(pre_act)
    mlp_term = jnp.dot(gelu_value.astype(BF16), mlp_out, preferred_element_type=F32)
    mlp_chunk = reduced_chunk(mlp_term.reshape(4, chunk_rows, vision_width))
    state_chunk = (image_float[:chunk_rows] + mlp_chunk).astype(BF16)
    image_state = gathered_chunks(state_chunk).reshape(image_rows, vision_width)

    partner_kv = swapped(jnp.stack([key_proj, value_proj]), "mp", 1)
    kv_cols = jnp.concatenate([key_proj, partner_kv[0], value_proj, partner_kv[1]], axis=1)
    local_kv = jnp.dot(image_state, kv_cols, preferred_element_type=F32).astype(BF16)
    both = jnp.stack([local_kv, swapped(local_kv, "group", 1)])
    by_y = {k: swapped(both, "seq", 2 * k) for k in FARTHEST_Y}
    own_core = jnp.stack([both, by_y[1], by_y[2], by_y[3]])
    other_core = swapped(own_core, "seq", 1)

    small = jax.ShapeDtypeStruct((text_rows, head_cols), BF16)
    wide = pltpu.VMEM((text_rows, text_width), BF16)
    queries, d_attended = pl.pallas_call(
        text_kernel,
        out_shape=(small, small),
        in_specs=[SMEM] + [VMEM] * 4 + [HBM] * 2,
        out_specs=(VMEM, VMEM),
        scratch_shapes=[wide] * 4 + [pltpu.SemaphoreType.DMA((2,))],
        compiler_params=SMALL_VMEM,
        name="text_projections",
    )(
        doc_image,
        attn_gate.reshape(1, 1),
        text_gain.reshape(1, text_width),
        *weights,
        *[pltpu.with_memory_space_constraint(x, pltpu.HBM) for x in (text_tokens, out_cotangent)],
    )

    grid = jax.ShapeDtypeStruct((2, 4, image_rows, 2 * HT), BF16)
    attended, grads_own, grads_other = pl.pallas_call(
        attend_kernel,
        out_shape=(small, grid, grid),
        in_specs=[SMEM] + [VMEM] * 4,
        out_specs=(VMEM, VMEM, VMEM),
        compiler_params=SMALL_VMEM,
        name="attention",
    )(doc_image, queries, d_attended, own_core, other_core)

    summed = grads_own.astype(F32) + swapped(grads_other, "seq", 1).astype(F32)
    summed = summed[0] + swapped(summed[1].astype(BF16), "group", 1).astype(F32)
    along_y = {k: swapped(summed[k].astype(BF16), "seq", 2 * k).astype(F32) for k in FARTHEST_Y}
    kv_grads = (summed[0] + along_y[1]) + (along_y[2] + along_y[3])
    state_term = contract_last(kv_grads.astype(BF16), kv_cols)
    state_chunk_grad = reduced_chunk(state_term.reshape(4, chunk_rows, vision_width))
    state_half = gathered_chunks(state_chunk_grad.astype(BF16)).reshape(image_rows, vision_width)
    d_hidden = contract_last(state_half, mlp_out)
    d_pre = (d_hidden * gelu_slope).astype(BF16)
    normed_term = contract_last(d_pre, mlp_in)
    d_normed = reduced_chunk(normed_term.reshape(4, chunk_rows, vision_width))
    grad_chunk = state_chunk_grad + norm_backward(
        d_normed, normed_hat[:chunk_rows], inv_scale[:chunk_rows], ln_gain
    )
    grads = gathered_chunks(grad_chunk.astype(BF16))
    image_grad = jnp.concatenate(
        [lax.dynamic_slice_in_dim(grads, near_index ^ k, 1, 0) for k in range(4)], axis=0
    ).reshape(image_rows, vision_width).astype(F32)

    terms = pl.pallas_call(
        term_kernel,
        out_shape=jax.ShapeDtypeStruct((16, text_rows, out_width), BF16),
        in_specs=[VMEM] * 3,
        out_specs=VMEM,
        compiler_params=SMALL_VMEM,
        name="text_terms",
    )(attended, *weights)
    terms = terms.reshape(4, 4, text_rows, out_width)
    kept, sent = pl.pallas_call(
        sum_kernel,
        out_shape=(
            jax.ShapeDtypeStruct((2, text_rows, out_width), F32),
            jax.ShapeDtypeStruct((2, text_rows, out_width), BF16),
        ),
        in_specs=[VMEM],
        out_specs=(VMEM, VMEM),
        compiler_params=SMALL_VMEM,
        name="near_sum",
    )(exchanged(terms, "mp", NEAR_SETS))
    passed = swapped(sent, "mp", 2).astype(F32)
    last = swapped((kept[1] + passed[1]).astype(BF16), "mp", 6).astype(F32)
    text_share = kept[0] + passed[0] + last
    text_slice = lax.dynamic_slice_in_dim(text_tokens, m * out_width, out_width, 1).astype(F32)
    has_image = jnp.where(doc_image[0] >= 0, 1.0, 0.0)
    text_out = (text_slice + jnp.tanh(attn_gate[0]) * has_image * text_share).astype(BF16)
    return (text_out, image_grad)


def solution(mesh):
    return jax.shard_map(
        shards,
        mesh=mesh,
        in_specs=(
            P(("group", "seq"), None),
            P(),
            P(),
            P(None, "mp"),
            P("mp", None),
            P(None, "mp"),
            P(None, "mp"),
            P(("group", "seq"), None),
            P(),
            P("seq", "mp"),
            P("seq", "mp"),
            P(),
            P(("group", "seq")),
            P(("group", "seq"), None),
        ),
        out_specs=(P(("group", "seq"), "mp"), P(("group", "seq"), None)),
        check_vma=False,
    )
```

```python
import jax
import jax.numpy as jnp
from jax import lax
from jax.experimental import pallas as pl
from jax.experimental.pallas import tpu as pltpu
from jax.sharding import PartitionSpec as P


HT = 128
EPS_VISION = 1e-06
EPS_TEXT = 1e-05
GELU_COEF = 0.7978845608028654
CUBIC_COEF = 0.044715

NEAR = (1, 8, 9)
FAR = (4, 2, 6)
FARTHEST_NEAR = (3, 1, 2)
FARTHEST_Y = (2, 1, 3)
NEAR_SETS = [[b, b + 1, b + 8, b + 9] for b in (0, 2, 4, 6)]
ALONG_Y = [[0, 2, 4, 6], [1, 3, 5, 7]]


F32 = jnp.float32
BF16 = jnp.bfloat16


def exchanged(x, axis, groups):
    return lax.all_to_all(x, axis, 0, 0, tiled=True, axis_index_groups=groups)


def swapped(x, axis, mask):
    return lax.ppermute(x, axis, [(i, i ^ mask) for i in range(lax.axis_size(axis))])


def gelu_parts(pre_act):
    cube_term = pre_act * pre_act * pre_act
    tangent = jnp.tanh(GELU_COEF * (pre_act + CUBIC_COEF * cube_term))
    gelu_value = 0.5 * pre_act * (1.0 + tangent)
    gelu_slope = 0.5 * (1.0 + tangent) + 0.5 * pre_act * (1.0 - tangent * tangent) * GELU_COEF * (
        1.0 + 3.0 * CUBIC_COEF * pre_act * pre_act
    )
    return (gelu_value, gelu_slope)


def vision_kernel(*refs):
    sources, outs, held, sems = refs[:5], refs[5:13], refs[13:18], refs[18]
    own, one, two, three, image_own, hat_own, inv_own, slope = outs
    image, gain, bias, mlp_in, mlp_out = held
    copies = [pltpu.make_async_copy(source, target, sems.at[i]) for i, (source, target) in enumerate(zip(sources, held))]
    for copy in copies:
        copy.start()
    m = lax.axis_index("mp")
    near = (m & 1) | ((m >> 3) << 1)
    rows = image.shape[0] // 4
    copies[0].wait()
    lines = [image[pl.ds(pl.multiple_of((near ^ k) * rows, rows), rows)] for k in range(4)]
    image_float = jnp.concatenate([x.astype(F32) for x in lines], axis=0)
    centred = image_float - jnp.mean(image_float, axis=1, keepdims=True)
    inv_scale = lax.rsqrt(jnp.mean(centred * centred, axis=1, keepdims=True) + EPS_VISION)
    normed_hat = centred * inv_scale
    copies[1].wait()
    copies[2].wait()
    normed = (normed_hat * gain[...][None, :] + bias[...][None, :]).astype(BF16)
    copies[3].wait()
    gelu_value, gelu_slope = gelu_parts(contract_last(normed, mlp_in[...]))
    copies[4].wait()
    term = jnp.dot(gelu_value.astype(BF16), mlp_out[...], preferred_element_type=F32)
    own[...] = term[:rows]
    for k, ref in enumerate((one, two, three)):
        ref[...] = term[(k + 1) * rows : (k + 2) * rows].astype(BF16)
    image_own[...] = image_float[:rows]
    hat_own[...] = normed_hat[:rows]
    inv_own[...] = jnp.broadcast_to(inv_scale[:rows], inv_own.shape)
    slope[...] = gelu_slope


def norm_backward(d_normed, normed_hat, inv_scale, ln_gain):
    scaled = d_normed * ln_gain
    first_mean = jnp.mean(scaled, axis=1, keepdims=True)
    second_mean = jnp.mean(scaled * normed_hat, axis=1, keepdims=True)
    return inv_scale * (scaled - first_mean - normed_hat * second_mean)


def contract_last(left, right):
    return lax.dot_general(left, right, (((1,), (1,)), ((), ())), preferred_element_type=F32)


def reduced_chunk(term):
    near = {k: swapped(term[k].astype(BF16), "mp", NEAR[k - 1]).astype(F32) for k in FARTHEST_NEAR}
    part = ((term[0] + near[1]) + (near[2] + near[3])).astype(BF16)
    far = [swapped(part, "mp", mask).astype(F32) for mask in FAR]
    return (part.astype(F32) + far[1]) + (far[0] + far[2])


def gathered_chunks(chunk):
    near = {k: swapped(chunk, "mp", NEAR[k - 1]) for k in FARTHEST_NEAR}
    return jnp.stack([chunk, near[1], near[2], near[3]])


def spread_kernel(first, second, out, held, sems):
    rows = first.shape[0]
    copies = [
        pltpu.make_async_copy(ref, held.at[pl.ds(i * rows, rows)], sems.at[i])
        for i, ref in enumerate((first, second))
    ]
    for copy in copies:
        copy.start()
    for copy in copies:
        copy.wait()
    copies = [pltpu.make_async_copy(held, out.at[i], sems.at[2 + i]) for i in range(out.shape[0])]
    for copy in copies:
        copy.start()
    for copy in copies:
        copy.wait()


def text_kernel(doc, gate, gain, own, other, tokens_in, cot_in, q_out, d_out, tokens, cot, normed, d_proj, sems):
    copies = [
        pltpu.make_async_copy(tokens_in, tokens, sems.at[0]),
        pltpu.make_async_copy(cot_in, cot, sems.at[1]),
    ]
    for copy in copies:
        copy.start()
    core = lax.axis_index("seq") & 1
    copies[0].wait()
    x = tokens[...].astype(F32)
    scale = lax.rsqrt(jnp.mean(x * x, axis=1, keepdims=True) + EPS_TEXT)
    normed[...] = (x * scale * gain[...]).astype(BF16)
    copies[1].wait()
    has_image = jnp.where(doc[0] >= 0, 1.0, 0.0)
    d_proj[...] = (jnp.tanh(gate[...]) * has_image * cot[...].astype(F32)).astype(BF16)
    rows, depth = tokens.shape[0], own.shape[1] // 2
    total_q = jnp.zeros((rows, q_out.shape[1]), F32)
    total_d = jnp.zeros((rows, d_out.shape[1]), F32)
    for y in range(own.shape[0]):
        for ref, side in ((own, core), (other, 1 - core)):
            cols = pl.ds(pl.multiple_of((2 * y + side) * depth, depth), depth)
            total_q += jnp.dot(normed[:, cols], ref[y, :depth], preferred_element_type=F32)
            total_d += jnp.dot(d_proj[:, cols], ref[y, depth:], preferred_element_type=F32)
    q_out[...] = total_q.astype(BF16)
    d_out[...] = total_d.astype(BF16)


def attend_kernel(doc, q, d, own, other, att_out, g_own, g_other):
    r = jnp.maximum(doc[0], 0) ^ lax.axis_index("group")
    peers, _, image_rows, _ = own.shape
    blocks = [ref[k, r] for ref in (own, other) for k in range(peers)]
    keys = jnp.concatenate([b[:, :HT] for b in blocks], axis=0)
    values = jnp.concatenate([b[:, HT:] for b in blocks], axis=0)
    head_scale = HT ** (-0.5)
    key_grads = jnp.zeros(keys.shape, F32)
    value_grads = jnp.zeros(keys.shape, F32)
    odd = (lax.axis_index("mp") & 1) == 1

    def turned(x):
        return jnp.where(odd, jnp.concatenate([x[:, HT // 2 :], x[:, : HT // 2]], axis=1), x)

    for h in range(q.shape[1] // HT):
        cols = slice(h * HT, (h + 1) * HT)
        qh, dh = turned(q[:, cols]), turned(d[:, cols])
        scores = contract_last(keys, qh) * head_scale
        expo = jnp.exp(scores - jnp.max(scores, axis=0, keepdims=True))
        soft = expo / jnp.sum(expo, axis=0, keepdims=True)
        half = soft.astype(BF16)
        att = lax.dot_general(half, values, (((0,), (0,)), ((), ())), preferred_element_type=F32)
        att_out[:, cols] = turned(att).astype(BF16)
        d_probs = contract_last(values, dh)
        delta = jnp.sum(half.astype(F32) * d_probs, axis=0, keepdims=True)
        d_scores = (soft * (d_probs - delta)).astype(BF16)
        value_grads += jnp.dot(half, dh, preferred_element_type=F32)
        key_grads += jnp.dot(d_scores, qh, preferred_element_type=F32)
    grads = jnp.concatenate([key_grads * head_scale, value_grads], axis=1).astype(BF16)
    nothing = jnp.zeros((image_rows, 2 * HT), BF16)
    for i, ref in enumerate((g_own, g_other)):
        for k in range(peers):
            at = (i * peers + k) * image_rows
            ref[r, k] = grads[at : at + image_rows]
            ref[1 - r, k] = nothing


def term_kernel(att, own, other, out):
    core, m = lax.axis_index("seq") & 1, lax.axis_index("mp")
    depth, width = own.shape[1] // 2, out.shape[2]
    for y in range(own.shape[0]):
        for ref, side in ((own, core), (other, 1 - core)):
            term = contract_last(att[...], ref[y, depth:]).astype(BF16)
            for half in range(depth // width):
                to = (2 * y + side) * (depth // width) + half
                near = (to & 1) | ((to >> 3) << 1)
                out[near * 4 + (((to ^ m) >> 1) & 3)] = term[:, half * width : (half + 1) * width]


def sum_kernel(arrived, kept, sent):
    for k in range(arrived.shape[1]):
        parts = [arrived[i, k].astype(F32) for i in range(arrived.shape[0])]
        total = (parts[0] + parts[1]) + (parts[2] + parts[3])
        if k in (1, 2):
            sent[k - 1] = total.astype(BF16)
        else:
            kept[k // 2] = total


VMEM = pl.BlockSpec(memory_space=pltpu.VMEM)
SMEM = pl.BlockSpec(memory_space=pltpu.SMEM)
HBM = pl.BlockSpec(memory_space=pltpu.HBM)
SMALL_VMEM = pltpu.CompilerParams(vmem_limit_bytes=16 * 1024 * 1024)


def shards(
    image_tokens,
    ln_gain,
    ln_bias,
    mlp_in,
    mlp_out,
    key_proj,
    value_proj,
    text_tokens,
    text_gain,
    query_proj,
    output_proj,
    attn_gate,
    doc_image,
    out_cotangent,
):
    m = lax.axis_index("mp")
    image_rows, vision_width = image_tokens.shape
    text_rows, text_width = text_tokens.shape
    out_width = text_width // lax.axis_size("mp")
    near_index = (m & 1) | ((m >> 3) << 1)
    chunk_rows = image_rows // 4

    depth, head_cols = query_proj.shape
    spread = pl.pallas_call(
        spread_kernel,
        out_shape=jax.ShapeDtypeStruct((4, 2 * depth, head_cols), BF16),
        in_specs=[HBM] * 2,
        out_specs=HBM,
        scratch_shapes=[pltpu.VMEM((2 * depth, head_cols), BF16), pltpu.SemaphoreType.DMA((6,))],
        compiler_params=SMALL_VMEM,
        name="spread",
    )(query_proj, output_proj)
    along = exchanged(spread, "seq", ALONG_Y)
    weights = [along, swapped(along, "seq", 1)]

    chunk = jax.ShapeDtypeStruct((chunk_rows, vision_width), F32)
    sent = jax.ShapeDtypeStruct((chunk_rows, vision_width), BF16)
    vision = (image_tokens, ln_gain, ln_bias, mlp_in.T, mlp_out)
    *mlp_term, image_own, hat_own, inv_own, gelu_slope = pl.pallas_call(
        vision_kernel,
        out_shape=(chunk, sent, sent, sent, chunk, chunk)
        + (jax.ShapeDtypeStruct((chunk_rows, HT), F32), jax.ShapeDtypeStruct((image_rows, mlp_in.shape[1]), F32)),
        in_specs=[HBM] * len(vision),
        out_specs=(VMEM,) * 8,
        scratch_shapes=[pltpu.VMEM(x.shape, x.dtype) for x in vision] + [pltpu.SemaphoreType.DMA((len(vision),))],
        compiler_params=SMALL_VMEM,
        name="vision",
    )(*[pltpu.with_memory_space_constraint(x, pltpu.HBM) for x in vision])
    state_chunk = (image_own + reduced_chunk(mlp_term)).astype(BF16)
    image_state = gathered_chunks(state_chunk).reshape(image_rows, vision_width)

    partner_kv = swapped(jnp.stack([key_proj, value_proj]), "mp", 1)
    kv_cols = jnp.concatenate([key_proj, partner_kv[0], value_proj, partner_kv[1]], axis=1)
    local_kv = jnp.dot(image_state, kv_cols, preferred_element_type=F32).astype(BF16)
    both = jnp.stack([local_kv, swapped(local_kv, "group", 1)])
    by_y = {k: swapped(both, "seq", 2 * k) for k in FARTHEST_Y}
    own_core = jnp.stack([both, by_y[1], by_y[2], by_y[3]])
    other_core = swapped(own_core, "seq", 1)

    small = jax.ShapeDtypeStruct((text_rows, head_cols), BF16)
    wide = pltpu.VMEM((text_rows, text_width), BF16)
    queries, d_attended = pl.pallas_call(
        text_kernel,
        out_shape=(small, small),
        in_specs=[SMEM] + [VMEM] * 4 + [HBM] * 2,
        out_specs=(VMEM, VMEM),
        scratch_shapes=[wide] * 4 + [pltpu.SemaphoreType.DMA((2,))],
        compiler_params=SMALL_VMEM,
        name="text_projections",
    )(
        doc_image,
        attn_gate.reshape(1, 1),
        text_gain.reshape(1, text_width),
        *weights,
        *[pltpu.with_memory_space_constraint(x, pltpu.HBM) for x in (text_tokens, out_cotangent)],
    )

    grid = jax.ShapeDtypeStruct((2, 4, image_rows, 2 * HT), BF16)
    attended, grads_own, grads_other = pl.pallas_call(
        attend_kernel,
        out_shape=(small, grid, grid),
        in_specs=[SMEM] + [VMEM] * 4,
        out_specs=(VMEM, VMEM, VMEM),
        compiler_params=SMALL_VMEM,
        name="attention",
    )(doc_image, queries, d_attended, own_core, other_core)

    summed = grads_own.astype(F32) + swapped(grads_other, "seq", 1).astype(F32)
    summed = summed[0] + swapped(summed[1].astype(BF16), "group", 1).astype(F32)
    along_y = {k: swapped(summed[k].astype(BF16), "seq", 2 * k).astype(F32) for k in FARTHEST_Y}
    kv_grads = (summed[0] + along_y[1]) + (along_y[2] + along_y[3])
    state_term = contract_last(kv_grads.astype(BF16), kv_cols)
    state_chunk_grad = reduced_chunk(state_term.reshape(4, chunk_rows, vision_width))
    state_half = gathered_chunks(state_chunk_grad.astype(BF16)).reshape(image_rows, vision_width)
    d_hidden = contract_last(state_half, mlp_out)
    d_pre = (d_hidden * gelu_slope).astype(BF16)
    normed_term = contract_last(d_pre, mlp_in)
    d_normed = reduced_chunk(normed_term.reshape(4, chunk_rows, vision_width))
    grad_chunk = state_chunk_grad + norm_backward(
        d_normed, hat_own, inv_own[:, :1], ln_gain
    )
    grads = gathered_chunks(grad_chunk.astype(BF16))
    image_grad = jnp.concatenate(
        [lax.dynamic_slice_in_dim(grads, near_index ^ k, 1, 0) for k in range(4)], axis=0
    ).reshape(image_rows, vision_width).astype(F32)

    terms = pl.pallas_call(
        term_kernel,
        out_shape=jax.ShapeDtypeStruct((16, text_rows, out_width), BF16),
        in_specs=[VMEM] * 3,
        out_specs=VMEM,
        compiler_params=SMALL_VMEM,
        name="text_terms",
    )(attended, *weights)
    terms = terms.reshape(4, 4, text_rows, out_width)
    kept, sent = pl.pallas_call(
        sum_kernel,
        out_shape=(
            jax.ShapeDtypeStruct((2, text_rows, out_width), F32),
            jax.ShapeDtypeStruct((2, text_rows, out_width), BF16),
        ),
        in_specs=[VMEM],
        out_specs=(VMEM, VMEM),
        compiler_params=SMALL_VMEM,
        name="near_sum",
    )(exchanged(terms, "mp", NEAR_SETS))
    passed = swapped(sent, "mp", 2).astype(F32)
    last = swapped((kept[1] + passed[1]).astype(BF16), "mp", 6).astype(F32)
    text_share = kept[0] + passed[0] + last
    text_slice = lax.dynamic_slice_in_dim(text_tokens, m * out_width, out_width, 1).astype(F32)
    has_image = jnp.where(doc_image[0] >= 0, 1.0, 0.0)
    text_out = (text_slice + jnp.tanh(attn_gate[0]) * has_image * text_share).astype(BF16)
    return (text_out, image_grad)


def solution(mesh):
    return jax.shard_map(
        shards,
        mesh=mesh,
        in_specs=(
            P(("group", "seq"), None),
            P(),
            P(),
            P(None, "mp"),
            P("mp", None),
            P(None, "mp"),
            P(None, "mp"),
            P(("group", "seq"), None),
            P(),
            P("seq", "mp"),
            P("seq", "mp"),
            P(),
            P(("group", "seq")),
            P(("group", "seq"), None),
        ),
        out_specs=(P(("group", "seq"), "mp"), P(("group", "seq"), None)),
        check_vma=False,
    )
```
